256 devices in a mesh: frames: 32 (over z_hi, y, x), rows: 2 (over core), batch: 4 (over z_lo).
Axes of the slice: x: 4, y: 4, z: 8 (z_hi: 2, z_lo: 4; z = z_hi * 4 + z_lo), core: 2. Of those that a mesh axis runs over, the one named last changes fastest.
Arguments:
- video: bfloat16 [256, 32, 128, 320], P(('batch', 'frames'), 'rows'), parts along dimension 0, may hold values from -6 to 6
- w_spatial: bfloat16 [3, 3, 320, 320], replicated, may hold values from -0.109375 to 0.109375
- b_spatial: float32 [320], replicated, may hold values from -3 to 3
- w_temporal: bfloat16 [3, 320, 320], replicated, may hold values from -0.1875 to 0.1875
- b_temporal: float32 [320], replicated, may hold values from -3 to 3
Outputs:
- downsampled: bfloat16 [128, 32, 128, 320], P(('batch', 'frames'), 'rows'), parts along dimension 0
The draws below stay inside these ranges and needn't reach their ends.
There are 4 independent parts, one for each index of `batch`. The reference program is written for one: setup_inputs(seed, part) draws one part's arguments, and reference() takes and returns one part's arrays. A program takes and returns all parts, laid end to end along the dimension named above; an argument that names none is the same for every part. Nothing has to cross between parts.
All inputs are finite; a program needn't handle non-finite values.
Results may differ from the reference program's by a relative error of at most 0.0042.
Values may be sent and summed in bfloat16 or wider, within the bound.
A program may use at most 64 MiB of HBM per device.

```python
import jax
import jax.numpy as jnp
from jax import lax

C = 320
W = 128
FRAMES = 64
H = 32


def levels(rng, dims, shards, least, top_value):
    factor_of = 1.0
    for dim, parts in shards:
        heights = jax.random.uniform(jax.random.fold_in(jax.random.fold_in(rng, 6), dim), (parts,), jnp.float32, least / len(shards), top_value / len(shards))
        factor_of = factor_of * jnp.repeat(jnp.exp(heights), dims[dim] // parts).reshape((-1,) + (1,) * (len(dims) - 1 - dim))
    return factor_of


def noise(stream_key, dims, spread, most, shards=(), held_as=jnp.bfloat16):
    loudness = levels(stream_key, dims, shards, -0.22, 0.18) if shards else 1.0
    drawn = jax.random.normal(stream_key, dims, jnp.float32) * spread * loudness
    return jnp.minimum(jnp.maximum(drawn, -most), most).astype(held_as)


def setup_inputs(seed: int = 0, part: int = 0) -> dict:
    key_list = jax.random.split(jax.random.key(seed), 6)
    part_splits = jax.random.split(jax.random.fold_in(key_list[5], part), 6)
    video = noise(part_splits[0], (FRAMES, H, W, C), 1.0, 6.0, ((0, 32), (1, 2)))
    w_spatial = noise(key_list[1], (3, 3, C, C), (9 * C) ** -0.5, 0.109375)
    b_spatial = noise(key_list[2], (C,), 0.5, 3.0, (), jnp.float32)
    w_temporal = noise(key_list[3], (3, C, C), (3 * C) ** -0.5, 0.1875)
    b_temporal = noise(key_list[4], (C,), 0.5, 3.0, (), jnp.float32)
    return {"video": video, "w_spatial": w_spatial, "b_spatial": b_spatial, "w_temporal": w_temporal, "b_temporal": b_temporal}


def reference(video, w_spatial, b_spatial, w_temporal, b_temporal):
    channels = video.shape[3]
    width = video.shape[2]
    height = video.shape[1]
    kernel = w_spatial.reshape(3, 3 * channels, channels)

    def spatial_frame(frame):
        padded = jnp.pad(frame, ((1, 1), (1, 1), (0, 0)))
        columns = jnp.concatenate([padded[:, 0:width], padded[:, 1:width + 1], padded[:, 2:width + 2]], axis=-1)
        summed = jnp.zeros((height, width, channels), jnp.float32) + b_spatial
        for row_tap in range(3):
            summed = summed + jnp.dot(columns[row_tap:row_tap + height], kernel[row_tap], preferred_element_type=jnp.float32)
        return jax.nn.silu(summed).astype(jnp.bfloat16)

    activated = lax.map(spatial_frame, video)
    even_frames = activated[0::2]
    odd_frames = activated[1::2]
    prev_frames = jnp.concatenate([jnp.zeros_like(odd_frames[:1]), odd_frames[:-1]], axis=0)
    total = jnp.dot(prev_frames, w_temporal[0], preferred_element_type=jnp.float32)
    total = total + jnp.dot(even_frames, w_temporal[1], preferred_element_type=jnp.float32)
    total = total + jnp.dot(odd_frames, w_temporal[2], preferred_element_type=jnp.float32)
    return (total + b_temporal).astype(jnp.bfloat16)
```

```python
import functools

import jax
import jax.numpy as jnp
from jax import lax
from jax.experimental import pallas as pl
from jax.experimental.pallas import tpu as pltpu
from jax.sharding import PartitionSpec as P

MESH = pl.DeviceIdType.MESH
F32 = jnp.float32
BF16 = jnp.bfloat16

LONG = (0, 2, 4, 6)
LONG_AT = (6, 9, 12, 15)
CROSS = {
    "direct": (13, 15),
    "a1": (5, 11),
    "b0": (0, 4, 8, 12),
    "b1": (1, 7),
    "c0": (2, 6, 10, 14),
    "c1": (3, 9),
}
CROSS_LAG = 4
LAST = ((1, 3), (5, 7), (8, 9), (0, 2), (10, 11), (12, 13), (4, 6), (14, 15))


def shifted_add(z, channels, width, lane):
    left, mid, right = z[:channels], z[channels : 2 * channels], z[2 * channels :]

    def roll(block, amount):
        return jnp.concatenate(
            [pltpu.roll(block[:, s * width : (s + 1) * width], amount, 1) for s in range(2)], axis=1
        )

    mid = mid + jnp.where(lane == 0, 0.0, roll(left, 1))
    return mid + jnp.where(lane == width - 1, 0.0, roll(right, width - 1))


def kernel(
    v_hbm, ws_hbm, bs_ref, wt_hbm, bt_ref, o_hbm,
    vbuf, wraw, traw, wmat, tmat, act, even, prev, acc, obuf, bias, longbuf, crossbuf,
    load_sem, halo_send, halo_recv, send_sem, prev_recv, long_recv, long_send, cross_recv, cross_send, out_sem,
):
    rows, channels, width = act.shape
    f, r, zl = lax.axis_index("frames"), lax.axis_index("rows"), lax.axis_index("batch")
    zh, y, x = f // 16, (f // 4) % 4, f % 4
    z = zh * 4 + zl
    turn = (z + 7 + 2 * (z % 2)) % 8
    source_z = turn

    def chip(cx, cy, cz):
        return (cz // 4 * 16 + cy * 4 + cx, r, cz % 4)

    def remote(src, dst, ssem, rsem, to):
        return pltpu.make_async_remote_copy(
            src_ref=src, dst_ref=dst, send_sem=ssem, recv_sem=rsem, device_id=to, device_id_type=MESH
        )

    odd_in = pltpu.make_async_copy(v_hbm.at[1], vbuf.at[1, pl.ds(1, rows)], load_sem.at[0])
    even_in = pltpu.make_async_copy(v_hbm.at[0], vbuf.at[0, pl.ds(1, rows)], load_sem.at[1])
    ws_in = pltpu.make_async_copy(ws_hbm, wraw, load_sem.at[2])
    wt_in = pltpu.make_async_copy(wt_hbm, traw, load_sem.at[3])
    ws_in.start()
    odd_in.start()
    even_in.start()
    wt_in.start()

    sends = jnp.logical_and(f != 15, f != 31)
    takes = jnp.logical_and(f != 0, f != 16)
    is_relay = x % 2 == 1
    far_origin = jnp.logical_not(jnp.logical_and(x == 1, y == 3))
    is_source = f == 15
    is_target = f == 16
    low = zh == 0
    turned = jnp.logical_or(jnp.logical_or(z == 7, z == 4), jnp.logical_or(z == 1, z == 2))
    corner_a = jnp.logical_and(x == 3, y == 3)
    corner_b = jnp.logical_and(x == 0, y == 3)
    corner_c = jnp.logical_and(x == 0, y == 0)
    roles = {
        "a1": jnp.logical_and(corner_a, turned),
        "b0": jnp.logical_and(corner_b, low),
        "b1": jnp.logical_and(corner_b, turned),
        "c0": jnp.logical_and(corner_c, low),
        "c1": jnp.logical_and(corner_c, turned),
    }
    spots = {"a1": (3, 3, 1), "b0": (0, 3, 0), "b1": (0, 3, 1), "c0": (0, 0, 0), "c1": (0, 0, 1)}
    next_frames = (f + 1, r, zl)
    sibling = (f, 1 - r, zl)
    relay = chip((x + 3 - x % 2) % 4, y, z)
    near_target = chip((x + 2) % 4, y, z)
    far_target = chip((x + 3) % 4, y + (3 - x) // 2, z)

    barrier = pltpu.get_barrier_semaphore()

    def tell(who):
        pl.semaphore_signal(barrier, inc=1, device_id=who, device_id_type=MESH)

    tell(sibling)

    @pl.when(takes)
    def _():
        before = f - 1
        bx, by = before % 4, (before // 4) % 4
        tell((before, r, zl))
        tell(chip((bx + 3 - bx % 2) % 4, by, z))

    @pl.when(is_relay)
    def _():
        tell(chip((x + 1) % 4, y, z))

    @pl.when(jnp.logical_and(is_relay, far_origin))
    def _():
        tell(chip((x + 2) % 4, y, z))

    for name, role in roles.items():

        @pl.when(role)
        def _(turned_here=spots[name][2]):
            tell(chip(3, 3, source_z if turned_here else z))

    @pl.when(is_target)
    def _():
        s = z - 4
        s_turn = (s + 7 + 2 * (s % 2)) % 8
        tell(chip(3, 3, s))
        for sx, sy, t in spots.values():
            tell(chip(sx, sy, s_turn if t else s))

    def count(condition, number=1):
        return condition.astype(jnp.int32) * number

    expected = 1 + count(sends, 2) + count(is_relay) + count(jnp.logical_and(is_relay, far_origin))
    expected = expected + count(is_source, 6)
    for role in roles.values():
        expected = expected + count(role)
    pl.semaphore_wait(barrier, expected)

    halos = [
        remote(
            v_hbm.at[i, (rows - 1) * (1 - r)],
            vbuf.at[i, (rows + 1) * r],
            halo_send.at[i],
            halo_recv.at[i],
            sibling,
        )
        for i in range(2)
    ]
    halos[1].start()
    halos[0].start()
    for i in range(2):
        vbuf[i, (rows + 1) * r] = jnp.zeros((channels, width), BF16)

    eye = lax.broadcasted_iota(jnp.int32, (channels, channels), 0) == lax.broadcasted_iota(
        jnp.int32, (channels, channels), 1
    )
    for i, ref in enumerate((bs_ref, bt_ref)):
        column = jnp.sum(jnp.where(eye, ref[...], 0.0), axis=1, keepdims=True)
        bias[i] = jnp.broadcast_to(column, (channels, 2 * width))

    ws_in.wait()
    for i in range(3):
        for j in range(3):
            wmat[j * channels : (j + 1) * channels, i * channels : (i + 1) * channels] = wraw[i, j].T
    odd_in.wait()
    halos[1].wait()

    lane = lax.broadcasted_iota(jnp.int32, (channels, 2 * width), 1) % width

    def spatial(i, h):
        lines = [vbuf[i, h + k] for k in range(4)]
        rhs = jnp.concatenate(
            [jnp.concatenate([lines[k], lines[k + 1]], axis=1) for k in range(3)], axis=0
        )
        total = jnp.dot(wmat[...], rhs, preferred_element_type=F32)
        total = shifted_add(total, channels, width, lane) + bias[0]
        return (total / (1.0 + jnp.exp(-total))).astype(BF16)

    def direct(h):
        return remote(act.at[h], prev.at[h], send_sem.at[h], prev_recv.at[h], next_frames)

    def long_first(k):
        return remote(
            act.at[LONG[k]], longbuf.at[x % 2, k], send_sem.at[LONG[k]], long_recv.at[x % 2, k], relay
        )

    def long_second(slot, k):
        to = far_target if slot else near_target
        return remote(
            longbuf.at[slot, k], prev.at[LONG[k]], long_send.at[slot, k], prev_recv.at[LONG[k]], to
        )

    def cross_first(name, h):
        if name == "direct":
            return remote(act.at[h], prev.at[h], send_sem.at[h], prev_recv.at[h], chip(0, 0, z + 4))
        sx, sy, t = spots[name]
        return remote(
            act.at[h], crossbuf.at[h], send_sem.at[h], cross_recv.at[h], chip(sx, sy, turn if t else z)
        )

    def cross_second(name, h):
        s = source_z if spots[name][2] else z
        return remote(crossbuf.at[h], prev.at[h], cross_send.at[h], prev_recv.at[h], chip(0, 0, s + 4))

    def first_sends(t):
        for h in (2 * t, 2 * t + 1):

            @pl.when(sends)
            def _(h=h):
                (long_first(LONG.index(h)) if h in LONG else direct(h)).start()

            @pl.when(is_source)
            def _(h=h):
                for name, taken in CROSS.items():
                    if h in taken:
                        cross_first(name, h).start()

    def second_sends(t):
        for k, at in enumerate(LONG_AT):
            if at == t:

                @pl.when(is_relay)
                def _(k=k):
                    pltpu.make_async_copy(longbuf.at[0, k], longbuf.at[0, k], long_recv.at[0, k]).wait()
                    long_second(0, k).start()

                @pl.when(jnp.logical_and(is_relay, far_origin))
                def _(k=k):
                    pltpu.make_async_copy(longbuf.at[1, k], longbuf.at[1, k], long_recv.at[1, k]).wait()
                    long_second(1, k).start()

        for name, role in roles.items():
            for h in CROSS[name]:
                if h // 2 + CROSS_LAG == t:

                    @pl.when(role)
                    def _(name=name, h=h):
                        pltpu.make_async_copy(crossbuf.at[h], crossbuf.at[h], cross_recv.at[h]).wait()
                        cross_second(name, h).start()

    @pl.loop(0, rows)
    def _(t):
        i = 1 - t // (rows // 2)
        h = t % (rows // 2) * 2

        @pl.when(t == rows // 2)
        def _():
            even_in.wait()
            halos[0].wait()

        out = spatial(i, h)

        @pl.when(i == 1)
        def _():
            act[h] = out[:, :width]
            act[h + 1] = out[:, width:]

        @pl.when(i == 0)
        def _():
            even[h] = out[:, :width]
            even[h + 1] = out[:, width:]

        for at in range(rows):

            @pl.when(t == at)
            def _(at=at):
                if at < rows // 2:
                    first_sends(at)
                second_sends(at)

    wt_in.wait()
    tmat[:, 0:channels] = traw[1].T
    tmat[:, channels : 2 * channels] = traw[2].T
    tmat[:, 2 * channels :] = traw[0].T

    @pl.loop(0, rows // 2)
    def _(t):
        h = t * 2
        rhs = jnp.concatenate(
            [
                jnp.concatenate([even[h], even[h + 1]], axis=1),
                jnp.concatenate([act[h], act[h + 1]], axis=1),
            ],
            axis=0,
        )
        part = jnp.dot(tmat[:, : 2 * channels], rhs, preferred_element_type=F32) + bias[1]
        acc[h] = part[:, :width]
        acc[h + 1] = part[:, width:]

    gets = f != 0
    for pair in LAST:
        for h in pair:

            @pl.when(gets)
            def _(h=h):
                pltpu.make_async_copy(prev.at[h], prev.at[h], prev_recv.at[h]).wait()

        a, b = pair

        @pl.when(gets)
        def _(a=a, b=b):
            rhs = jnp.concatenate([prev[a], prev[b]], axis=1)
            part = jnp.dot(tmat[:, 2 * channels :], rhs, preferred_element_type=F32)
            obuf[a] = (acc[a] + part[:, :width]).astype(BF16)
            obuf[b] = (acc[b] + part[:, width:]).astype(BF16)

        @pl.when(jnp.logical_not(gets))
        def _(a=a, b=b):
            obuf[a] = acc[a].astype(BF16)
            obuf[b] = acc[b].astype(BF16)

        for h in pair:
            pltpu.make_async_copy(obuf.at[h], o_hbm.at[h], out_sem.at[h]).start()

    @pl.when(sends)
    def _():
        for h in range(rows):
            direct(h).wait_send()

    @pl.when(is_source)
    def _():
        for h in range(rows):
            direct(h).wait_send()

    for k in range(len(LONG)):

        @pl.when(is_relay)
        def _(k=k):
            long_second(0, k).wait_send()

        @pl.when(jnp.logical_and(is_relay, far_origin))
        def _(k=k):
            long_second(1, k).wait_send()

    for name, role in roles.items():
        for h in CROSS[name]:

            @pl.when(role)
            def _(name=name, h=h):
                cross_second(name, h).wait_send()

    for h in range(rows):
        pltpu.make_async_copy(obuf.at[h], o_hbm.at[h], out_sem.at[h]).wait()


def per_device(video, w_spatial, b_spatial, w_temporal, b_temporal):
    frames, rows, width, channels = video.shape
    dma = pltpu.SemaphoreType.DMA
    out = pl.pallas_call(
        kernel,
        out_shape=jax.ShapeDtypeStruct((rows, channels, width), BF16),
        in_specs=[
            pl.BlockSpec(memory_space=pl.ANY),
            pl.BlockSpec(memory_space=pl.ANY),
            pl.BlockSpec(memory_space=pltpu.VMEM),
            pl.BlockSpec(memory_space=pl.ANY),
            pl.BlockSpec(memory_space=pltpu.VMEM),
        ],
        out_specs=pl.BlockSpec(memory_space=pl.ANY),
        scratch_shapes=[
            pltpu.VMEM((frames, rows + 2, channels, width), BF16),
            pltpu.VMEM(w_spatial.shape, BF16),
            pltpu.VMEM(w_temporal.shape, BF16),
            pltpu.VMEM((3 * channels, 3 * channels), BF16),
            pltpu.VMEM((channels, 3 * channels), BF16),
            pltpu.VMEM((rows, channels, width), BF16),
            pltpu.VMEM((rows, channels, width), BF16),
            pltpu.VMEM((rows, channels, width), BF16),
            pltpu.VMEM((rows, channels, width), F32),
            pltpu.VMEM((rows, channels, width), BF16),
            pltpu.VMEM((2, channels, 2 * width), F32),
            pltpu.VMEM((2, len(LONG), channels, width), BF16),
            pltpu.VMEM((rows, channels, width), BF16),
            dma((4,)),
            dma((2,)),
            dma((2,)),
            dma((rows,)),
            dma((rows,)),
            dma((2, len(LONG))),
            dma((2, len(LONG))),
            dma((rows,)),
            dma((rows,)),
            dma((rows,)),
        ],
        compiler_params=pltpu.CompilerParams(
            collective_id=0, has_side_effects=True, vmem_limit_bytes=60 * 1024 * 1024
        ),
        name="level",
    )(
        jnp.swapaxes(video, 2, 3),
        w_spatial,
        b_spatial,
        w_temporal,
        b_temporal,
    )
    return jnp.swapaxes(out, 1, 2)[None]


def solution(mesh):
    in_specs = (P(("batch", "frames"), "rows", None, None), P(), P(), P(), P())
    out_specs = P(("batch", "frames"), "rows", None, None)
    return jax.shard_map(
        per_device, mesh=mesh, in_specs=in_specs, out_specs=out_specs, check_vma=False
    )
```

```python
import functools

import jax
import jax.numpy as jnp
from jax import lax
from jax.experimental import pallas as pl
from jax.experimental.pallas import tpu as pltpu
from jax.sharding import PartitionSpec as P

SPAN = 4
MAIN = 256
ONES = 16
GROUP = 16
MESH = pl.DeviceIdType.MESH
F32 = jnp.float32
BF16 = jnp.bfloat16

STEPS = ((1, 4), (1, 8), (1, 0), (1, 12), (0, 4), (0, 8), (0, 0), (0, 12))
LONG = (4, 6, 8, 10)
CROSS = {
    "direct": (8, 10, 3, 12, 15),
    "c1": (4,),
    "b0": (6, 13),
    "c0": (9, 0, 2, 14),
    "e0": (5, 7, 11, 1),
}
BETWEEN = {
    4: (("long", (0, 0)), ("cross", (4, 5))),
    5: (("long", (0, 1)), ("cross", (6,))),
    6: (("long", (0, 2)),),
    7: (("long", (0, 3)), ("cross", (7, 9))),
}
AFTER = (
    ("long", (1, 0)), ("pair", (5, 7)), ("pair", (9, 11)), ("cross", (11,)), ("long", (1, 1)), ("pair", (0, 1)),
    ("cross", (0,)), ("long", (1, 2)), ("cross", (1,)), ("long", (1, 3)), ("pair", (2, 3)), ("cross", (2, 13)),
    ("pair", (12, 13)), ("pair", (4, 6)), ("cross", (14,)), ("pair", (8, 10)), ("pair", (14, 15)),
)


def shifted_add(z, channels, width, lane):
    left, mid, right = (z[:, j].reshape(channels, SPAN * width) for j in range(3))

    def roll(block, amount):
        return jnp.concatenate(
            [pltpu.roll(block[:, s * width : (s + 1) * width], amount, 1) for s in range(SPAN)], axis=1
        )

    mid = mid + jnp.where(lane == 0, 0.0, roll(left, 1))
    return mid + jnp.where(lane == width - 1, 0.0, roll(right, width - 1))


def kernel(
    v_hbm, ws_hbm, bs_ref, wt_hbm, bt_ref, o_hbm,
    vbuf, wraw, traw, wmat, tmat, act, even, prev, obuf, za, zb, longbuf, crossbuf,
    load_sem, halo_send, halo_recv, send_sem, prev_recv, long_recv, long_send, cross_recv, cross_send, out_sem,
):
    rows, channels, width = act.shape
    groups = channels // GROUP
    f, r, zl = lax.axis_index("frames"), lax.axis_index("rows"), lax.axis_index("batch")
    zh, y, x = f // 16, (f // 4) % 4, f % 4
    z = zh * 4 + zl
    turn = (z + 7 + 2 * (z % 2)) % 8
    source_z = turn

    def chip(cx, cy, cz):
        return (cz // 4 * 16 + cy * 4 + cx, r, cz % 4)

    def remote(src, dst, ssem, rsem, to):
        return pltpu.make_async_remote_copy(
            src_ref=src, dst_ref=dst, send_sem=ssem, recv_sem=rsem, device_id=to, device_id_type=MESH
        )

    ws_in = [
        pltpu.make_async_copy(ws_hbm.at[:, j], wraw.at[:, j], load_sem.at[j]) for j in range(3)
    ]
    odd_in = pltpu.make_async_copy(v_hbm.at[1], vbuf.at[1, pl.ds(1, rows)], load_sem.at[3])
    even_in = pltpu.make_async_copy(v_hbm.at[0], vbuf.at[0, pl.ds(1, rows)], load_sem.at[4])
    wt_in = pltpu.make_async_copy(wt_hbm, traw, load_sem.at[5])
    for copy in (ws_in[0], ws_in[1], ws_in[2], odd_in, even_in, wt_in):
        copy.start()

    sends = jnp.logical_and(f != 15, f != 31)
    takes = jnp.logical_and(f != 0, f != 16)
    first_relay = jnp.logical_not(jnp.logical_and(x == 2, y == 0))
    second_relay = jnp.logical_not(jnp.logical_and(x == 1, y == 0))
    is_source = f == 15
    is_target = f == 16
    low = zh == 0
    turned = jnp.logical_or(jnp.logical_or(z == 7, z == 4), jnp.logical_or(z == 1, z == 2))
    corner_b = jnp.logical_and(x == 0, y == 3)
    corner_c = jnp.logical_and(x == 0, y == 0)
    corner_e = jnp.logical_and(x == 0, y == 1)
    roles = {
        "c1": jnp.logical_and(corner_c, turned),
        "b0": jnp.logical_and(corner_b, low),
        "c0": jnp.logical_and(corner_c, low),
        "e0": jnp.logical_and(corner_e, low),
    }
    spots = {"c1": (0, 0, 1), "b0": (0, 3, 0), "c0": (0, 0, 0), "e0": (0, 1, 0)}
    next_frames = (f + 1, r, zl)
    sibling = (f, 1 - r, zl)
    left = chip((x + 3) % 4, y, z)
    right = chip((x + 1) % 4, y, z)
    long_start = chip((x + 3) % 4, y + x // 3, z)
    long_origin = chip((x + 1) % 4, y - (x + 1) % 4 // 3, z)

    barrier = pltpu.get_barrier_semaphore()

    def tell(who):
        pl.semaphore_signal(barrier, inc=1, device_id=who, device_id_type=MESH)

    tell(sibling)

    @pl.when(takes)
    def _():
        tell((f - 1, r, zl))
        tell(right)

    @pl.when(first_relay)
    def _():
        tell(long_origin)

    @pl.when(second_relay)
    def _():
        tell(right)

    for name, role in roles.items():

        @pl.when(role)
        def _(turned_here=spots[name][2]):
            tell(chip(3, 3, source_z if turned_here else z))

    @pl.when(is_target)
    def _():
        s = z - 4
        s_turn = (s + 7 + 2 * (s % 2)) % 8
        tell(chip(3, 3, s))
        for sx, sy, t in spots.values():
            tell(chip(sx, sy, s_turn if t else s))

    def count(condition, number=1):
        return condition.astype(jnp.int32) * number

    expected = 1 + count(sends, 2) + count(first_relay) + count(second_relay)
    expected = expected + count(is_source, 1 + len(roles))
    for role in roles.values():
        expected = expected + count(role)
    def turned_about(blocks, bias_ref):
        if bias_ref is None:
            last = jnp.zeros((ONES, channels), BF16)
        else:
            parts, left = [], jnp.reshape(bias_ref[...], (1, channels))
            for _ in range(3):
                parts.append(left.astype(BF16).astype(F32))
                left = left - parts[-1]
            row = lax.broadcasted_iota(jnp.int32, (ONES, channels), 0)
            last = jnp.zeros((ONES, channels), F32)
            for k, part in enumerate(parts):
                last = jnp.where(row == k, jnp.broadcast_to(part, (ONES, channels)), last)
            last = last.astype(BF16)
        for block in blocks:
            yield block[:MAIN].T
        yield jnp.concatenate([block[MAIN:] for block in blocks] + [last], axis=0).T

    for j in range(3):
        ws_in[j].wait()
        blocks = [wraw.at[i, j] for i in range(3)]
        at = 0
        for piece in turned_about(blocks, bs_ref if j == 1 else None):
            size = piece.shape[1]
            wmat[:, j, :, at : at + size] = piece.reshape(groups, GROUP, size)
            at += size

    pl.semaphore_wait(barrier, expected)
    halos = [
        remote(
            v_hbm.at[i, (rows - 1) * (1 - r)],
            vbuf.at[i, (rows + 1) * r],
            halo_send.at[i],
            halo_recv.at[i],
            sibling,
        )
        for i in range(2)
    ]
    halos[1].start()
    halos[0].start()
    for i in range(2):
        vbuf[i, (rows + 1) * r] = jnp.zeros((channels, width), BF16)
    odd_in.wait()

    lane = lax.broadcasted_iota(jnp.int32, (channels, SPAN * width), 1) % width
    depth = 3 * channels + ONES

    def stacked(rows_of):
        columns = len(rows_of) * width
        ones = (lax.broadcasted_iota(jnp.int32, (ONES, columns), 0) < 3).astype(F32).astype(BF16)
        return jnp.concatenate(
            [
                jnp.concatenate([lines[k][part] for lines in rows_of], axis=1)
                for part in (slice(0, MAIN), slice(MAIN, None))
                for k in range(3)
            ]
            + [ones],
            axis=0,
        )

    def taps(i, h):
        lines = [vbuf[i, h + k] for k in range(SPAN + 2)]
        return jnp.dot(
            wmat[...].reshape(3 * channels, depth),
            stacked([lines[k : k + 3] for k in range(SPAN)]),
            preferred_element_type=F32,
        )

    def finish(taken, out, h):
        total = shifted_add(taken.reshape(groups, 3, GROUP, SPAN * width), channels, width, lane)
        total = (total / (1.0 + jnp.exp(-total))).astype(BF16)
        for k in range(SPAN):
            out[h + k] = total[:, k * width : (k + 1) * width]

    def direct(h):
        return remote(act.at[h], prev.at[h], send_sem.at[h], prev_recv.at[h], next_frames)

    def long_first(k):
        h = LONG[k]
        return remote(act.at[h], longbuf.at[0, k], send_sem.at[h], long_recv.at[0, k], long_start)

    def long_next(stage, k):
        there, arrived = (
            (longbuf.at[1, k], long_recv.at[1, k]) if stage == 0 else (prev.at[LONG[k]], prev_recv.at[LONG[k]])
        )
        return remote(longbuf.at[stage, k], there, long_send.at[stage, k], arrived, left)

    def cross_first(name, h):
        if name == "direct":
            return remote(act.at[h], prev.at[h], send_sem.at[h], prev_recv.at[h], chip(0, 0, z + 4))
        sx, sy, t = spots[name]
        return remote(
            act.at[h], crossbuf.at[h], send_sem.at[h], cross_recv.at[h], chip(sx, sy, turn if t else z)
        )

    def cross_second(name, h):
        s = source_z if spots[name][2] else z
        return remote(crossbuf.at[h], prev.at[h], cross_send.at[h], prev_recv.at[h], chip(0, 0, s + 4))

    def first_sends(first):
        for h in range(first, first + SPAN):

            @pl.when(sends)
            def _(h=h):
                (long_first(LONG.index(h)) if h in LONG else direct(h)).start()

            @pl.when(is_source)
            def _(h=h):
                for name, taken in CROSS.items():
                    if h in taken:
                        cross_first(name, h).start()

    def long_pass(stage, k):
        @pl.when((first_relay, second_relay)[stage])
        def _():
            pltpu.make_async_copy(longbuf.at[stage, k], longbuf.at[stage, k], long_recv.at[stage, k]).wait()
            long_next(stage, k).start()

    def cross_pass(taken):
        for name, role in roles.items():
            mine = [h for h in taken if h in CROSS[name]]
            if mine:

                @pl.when(role)
                def _(name=name, mine=mine):
                    for h in mine:
                        pltpu.make_async_copy(crossbuf.at[h], crossbuf.at[h], cross_recv.at[h]).wait()
                        cross_second(name, h).start()

    def temporal(pair):
        @pl.when(gets)
        def _():
            for h in pair:
                pltpu.make_async_copy(prev.at[h], prev.at[h], prev_recv.at[h]).wait()

        rhs = stacked([[ref[h] for ref in (prev, even, act)] for h in pair])
        total = jnp.dot(tmat[...], rhs, preferred_element_type=F32).astype(BF16)
        for k, h in enumerate(pair):
            obuf[h] = total[:, k * width : (k + 1) * width]
            pltpu.make_async_copy(obuf.at[h], o_hbm.at[h], out_sem.at[h]).start()

    finish(taps(*STEPS[0]), act, STEPS[0][1])
    first_sends(STEPS[0][1])
    za[...] = taps(*STEPS[1])
    here, there = za, zb
    for n in range(2, len(STEPS) + 1):
        if n < len(STEPS):
            if STEPS[n][1] in (0, rows - SPAN) and STEPS[n - 1][1] not in (0, rows - SPAN):
                halos[STEPS[n][0]].wait_recv()
            if STEPS[n][0] != STEPS[n - 1][0]:
                even_in.wait()
            there[...] = taps(*STEPS[n])
        else:
            wt_in.wait()
            at = 0
            for piece in turned_about([traw.at[k] for k in range(3)], bt_ref):
                tmat[:, at : at + piece.shape[1]] = piece
                at += piece.shape[1]
        i, h = STEPS[n - 1]
        finish(here[...], act if i else even, h)
        if i:
            first_sends(h)
        here, there = there, here
        for kind, what in BETWEEN.get(n, ()):
            if kind == "long":
                long_pass(*what)
            else:
                cross_pass(what)

    @pl.when(f == 0)
    def _():
        prev[...] = jnp.zeros_like(prev)

    gets = f != 0
    for kind, what in AFTER:
        if kind == "long":
            long_pass(*what)
        elif kind == "cross":
            cross_pass(what)
        else:

            @pl.when(jnp.logical_not(is_target))
            def _(what=what):
                temporal(what)

    @pl.when(is_target)
    def _():
        @pl.loop(0, rows // 2)
        def _(t):
            inner = jnp.logical_and(t >= 4, t < 6).astype(jnp.int32)
            h = 2 * t + 4 - 12 * inner - 4 * (t >= 6).astype(jnp.int32)
            temporal((h, h + 1))

    for i in range(2):
        halos[i].wait_send()

    @pl.when(sends)
    def _():
        for h in range(rows):
            direct(h).wait_send()

    @pl.when(is_source)
    def _():
        for h in range(rows):
            direct(h).wait_send()

    for stage, role in enumerate((first_relay, second_relay)):

        @pl.when(role)
        def _(stage=stage):
            for k in range(len(LONG)):
                long_next(stage, k).wait_send()

    for name, role in roles.items():
        for h in CROSS[name]:

            @pl.when(role)
            def _(name=name, h=h):
                cross_second(name, h).wait_send()

    for h in range(rows):
        pltpu.make_async_copy(obuf.at[h], o_hbm.at[h], out_sem.at[h]).wait()


def per_device(video, w_spatial, b_spatial, w_temporal, b_temporal):
    frames, rows, width, channels = video.shape
    dma = pltpu.SemaphoreType.DMA
    out = pl.pallas_call(
        kernel,
        out_shape=jax.ShapeDtypeStruct((rows, channels, width), BF16),
        in_specs=[
            pl.BlockSpec(memory_space=pl.ANY),
            pl.BlockSpec(memory_space=pl.ANY),
            pl.BlockSpec(memory_space=pltpu.VMEM),
            pl.BlockSpec(memory_space=pl.ANY),
            pl.BlockSpec(memory_space=pltpu.VMEM),
        ],
        out_specs=pl.BlockSpec(memory_space=pl.ANY),
        scratch_shapes=[
            pltpu.VMEM((frames, rows + 2, channels, width), BF16),
            pltpu.VMEM(w_spatial.shape, BF16),
            pltpu.VMEM(w_temporal.shape, BF16),
            pltpu.VMEM((channels // GROUP, 3, GROUP, 3 * channels + ONES), BF16),
            pltpu.VMEM((channels, 3 * channels + ONES), BF16),
            pltpu.VMEM((rows, channels, width), BF16),
            pltpu.VMEM((rows, channels, width), BF16),
            pltpu.VMEM((rows, channels, width), BF16),
            pltpu.VMEM((rows, channels, width), BF16),
            pltpu.VMEM((3 * channels, SPAN * width), F32),
            pltpu.VMEM((3 * channels, SPAN * width), F32),
            pltpu.VMEM((2, len(LONG), channels, width), BF16),
            pltpu.VMEM((rows, channels, width), BF16),
            dma((6,)),
            dma((2,)),
            dma((2,)),
            dma((rows,)),
            dma((rows,)),
            dma((2, len(LONG))),
            dma((2, len(LONG))),
            dma((rows,)),
            dma((rows,)),
            dma((rows,)),
        ],
        compiler_params=pltpu.CompilerParams(
            collective_id=0, has_side_effects=True, vmem_limit_bytes=60 * 1024 * 1024
        ),
        name="level",
    )(
        jnp.swapaxes(video, 2, 3),
        w_spatial,
        b_spatial,
        w_temporal,
        b_temporal,
    )
    return jnp.swapaxes(out, 1, 2)[None]


def solution(mesh):
    in_specs = (P(("batch", "frames"), "rows", None, None), P(), P(), P(), P())
    out_specs = P(("batch", "frames"), "rows", None, None)
    return jax.shard_map(
        per_device, mesh=mesh, in_specs=in_specs, out_specs=out_specs, check_vma=False
    )
```

```python
import functools

import jax
import jax.numpy as jnp
from jax import lax
from jax.experimental import pallas as pl
from jax.experimental.pallas import tpu as pltpu
from jax.sharding import PartitionSpec as P

SPAN = 4
MAIN = 256
ONES = 16
GROUP = 16
MESH = pl.DeviceIdType.MESH
F32 = jnp.float32
BF16 = jnp.bfloat16

STEPS = ((1, 4), (1, 8), (1, 0), (1, 12), (0, 4), (0, 8), (0, 0), (0, 12))
LONG = (4, 6, 8, 10)
CROSS = {
    "direct": (8, 10, 3, 12, 15),
    "c1": (4,),
    "b0": (6, 13),
    "c0": (9, 0, 2),
    "e0": (5, 7, 11, 1, 14),
}
BETWEEN = {
    4: (("long", (0, 0)), ("cross", (4, 5))),
    5: (("long", (0, 1)), ("cross", (6,))),
    6: (("long", (0, 2)),),
    7: (("long", (0, 3)), ("cross", (7, 9))),
}
AFTER = (
    ("long", (1, 0)), ("pair", (5, 7)), ("pair", (9, 11)), ("cross", (11,)), ("long", (1, 1)), ("pair", (0, 1)),
    ("cross", (0,)), ("long", (1, 2)), ("cross", (1,)), ("long", (1, 3)), ("pair", (2, 3)), ("cross", (2, 13)),
    ("pair", (12, 13)), ("pair", (4, 6)), ("cross", (14,)), ("pair", (8, 10)), ("pair", (14, 15)),
)


def shifted_add(z, channels, width, lane):
    left, mid, right = (z[:, j].reshape(channels, SPAN * width) for j in range(3))

    def roll(block, amount):
        return jnp.concatenate(
            [pltpu.roll(block[:, s * width : (s + 1) * width], amount, 1) for s in range(SPAN)], axis=1
        )

    mid = mid + jnp.where(lane == 0, 0.0, roll(left, 1))
    return mid + jnp.where(lane == width - 1, 0.0, roll(right, width - 1))


def kernel(
    v_hbm, ws_hbm, bs_ref, wt_hbm, bt_ref, o_ref,
    vbuf, wraw, traw, wmat, tmat, act, even, prev, za, zb, longbuf, crossbuf,
    load_sem, halo_send, halo_recv, send_sem, prev_recv, long_recv, long_send, cross_recv, cross_send,
):
    rows, channels, width = act.shape
    groups = channels // GROUP
    f, r, zl = lax.axis_index("frames"), lax.axis_index("rows"), lax.axis_index("batch")
    zh, y, x = f // 16, (f // 4) % 4, f % 4
    z = zh * 4 + zl
    turn = (z + 7 + 2 * (z % 2)) % 8
    source_z = turn

    def chip(cx, cy, cz):
        return (cz // 4 * 16 + cy * 4 + cx, r, cz % 4)

    def remote(src, dst, ssem, rsem, to):
        return pltpu.make_async_remote_copy(
            src_ref=src, dst_ref=dst, send_sem=ssem, recv_sem=rsem, device_id=to, device_id_type=MESH
        )

    ws_in = [
        pltpu.make_async_copy(ws_hbm.at[:, j], wraw.at[:, j], load_sem.at[j]) for j in range(3)
    ]
    odd_in = pltpu.make_async_copy(v_hbm.at[1], vbuf.at[1, pl.ds(1, rows)], load_sem.at[3])
    even_in = pltpu.make_async_copy(v_hbm.at[0], vbuf.at[0, pl.ds(1, rows)], load_sem.at[4])
    wt_in = pltpu.make_async_copy(wt_hbm, traw, load_sem.at[5])
    for copy in (ws_in[0], ws_in[1], ws_in[2], odd_in, even_in, wt_in):
        copy.start()

    sends = jnp.logical_and(f != 15, f != 31)
    takes = jnp.logical_and(f != 0, f != 16)
    first_relay = jnp.logical_not(jnp.logical_and(x == 2, y == 0))
    second_relay = jnp.logical_not(jnp.logical_and(x == 1, y == 0))
    is_source = f == 15
    is_target = f == 16
    low = zh == 0
    turned = jnp.logical_or(jnp.logical_or(z == 7, z == 4), jnp.logical_or(z == 1, z == 2))
    corner_b = jnp.logical_and(x == 0, y == 3)
    corner_c = jnp.logical_and(x == 0, y == 0)
    corner_e = jnp.logical_and(x == 0, y == 1)
    roles = {
        "c1": jnp.logical_and(corner_c, turned),
        "b0": jnp.logical_and(corner_b, low),
        "c0": jnp.logical_and(corner_c, low),
        "e0": jnp.logical_and(corner_e, low),
    }
    spots = {"c1": (0, 0, 1), "b0": (0, 3, 0), "c0": (0, 0, 0), "e0": (0, 1, 0)}
    next_frames = (f + 1, r, zl)
    sibling = (f, 1 - r, zl)
    left = chip((x + 3) % 4, y, z)
    right = chip((x + 1) % 4, y, z)
    long_start = chip((x + 3) % 4, y + x // 3, z)
    long_origin = chip((x + 1) % 4, y - (x + 1) % 4 // 3, z)

    barrier = pltpu.get_barrier_semaphore()

    def tell(who):
        pl.semaphore_signal(barrier, inc=1, device_id=who, device_id_type=MESH)

    tell(sibling)

    @pl.when(takes)
    def _():
        tell((f - 1, r, zl))
        tell(right)

    @pl.when(first_relay)
    def _():
        tell(long_origin)

    @pl.when(second_relay)
    def _():
        tell(right)

    for name, role in roles.items():

        @pl.when(role)
        def _(turned_here=spots[name][2]):
            tell(chip(3, 3, source_z if turned_here else z))

    @pl.when(is_target)
    def _():
        s = z - 4
        s_turn = (s + 7 + 2 * (s % 2)) % 8
        tell(chip(3, 3, s))
        for sx, sy, t in spots.values():
            tell(chip(sx, sy, s_turn if t else s))

    def count(condition, number=1):
        return condition.astype(jnp.int32) * number

    expected = 1 + count(sends, 2) + count(first_relay) + count(second_relay)
    expected = expected + count(is_source, 1 + len(roles))
    for role in roles.values():
        expected = expected + count(role)
    def turned_about(blocks, bias_ref):
        if bias_ref is None:
            last = jnp.zeros((ONES, channels), BF16)
        else:
            parts, left = [], jnp.reshape(bias_ref[...], (1, channels))
            for _ in range(3):
                parts.append(left.astype(BF16).astype(F32))
                left = left - parts[-1]
            row = lax.broadcasted_iota(jnp.int32, (ONES, channels), 0)
            last = jnp.zeros((ONES, channels), F32)
            for k, part in enumerate(parts):
                last = jnp.where(row == k, jnp.broadcast_to(part, (ONES, channels)), last)
            last = last.astype(BF16)
        for block in blocks:
            yield block[:MAIN].T
        yield jnp.concatenate([block[MAIN:] for block in blocks] + [last], axis=0).T

    for j in range(3):
        ws_in[j].wait()
        blocks = [wraw.at[i, j] for i in range(3)]
        at = 0
        for piece in turned_about(blocks, bs_ref if j == 1 else None):
            size = piece.shape[1]
            wmat[:, j, :, at : at + size] = piece.reshape(groups, GROUP, size)
            at += size

    pl.semaphore_wait(barrier, expected)
    halos = [
        remote(
            v_hbm.at[i, (rows - 1) * (1 - r)],
            vbuf.at[i, (rows + 1) * r],
            halo_send.at[i],
            halo_recv.at[i],
            sibling,
        )
        for i in range(2)
    ]
    halos[1].start()
    halos[0].start()
    for i in range(2):
        vbuf[i, (rows + 1) * r] = jnp.zeros((channels, width), BF16)
    odd_in.wait()

    lane = lax.broadcasted_iota(jnp.int32, (channels, SPAN * width), 1) % width
    depth = 3 * channels + ONES

    def stacked(rows_of):
        columns = len(rows_of) * width
        ones = (lax.broadcasted_iota(jnp.int32, (ONES, columns), 0) < 3).astype(F32).astype(BF16)
        return jnp.concatenate(
            [
                jnp.concatenate([lines[k][part] for lines in rows_of], axis=1)
                for part in (slice(0, MAIN), slice(MAIN, None))
                for k in range(3)
            ]
            + [ones],
            axis=0,
        )

    def taps(i, h):
        lines = [vbuf[i, h + k] for k in range(SPAN + 2)]
        return jnp.dot(
            wmat[...].reshape(3 * channels, depth),
            stacked([lines[k : k + 3] for k in range(SPAN)]),
            preferred_element_type=F32,
        )

    def finish(taken, out, h):
        total = shifted_add(taken.reshape(groups, 3, GROUP, SPAN * width), channels, width, lane)
        total = (total / (1.0 + jnp.exp(-total))).astype(BF16)
        for k in range(SPAN):
            out[h + k] = total[:, k * width : (k + 1) * width]

    def direct(h):
        return remote(act.at[h], prev.at[h], send_sem.at[h], prev_recv.at[h], next_frames)

    def long_first(k):
        h = LONG[k]
        return remote(act.at[h], longbuf.at[0, k], send_sem.at[h], long_recv.at[0, k], long_start)

    def long_next(stage, k):
        there, arrived = (
            (longbuf.at[1, k], long_recv.at[1, k]) if stage == 0 else (prev.at[LONG[k]], prev_recv.at[LONG[k]])
        )
        return remote(longbuf.at[stage, k], there, long_send.at[stage, k], arrived, left)

    def cross_first(name, h):
        if name == "direct":
            return remote(act.at[h], prev.at[h], send_sem.at[h], prev_recv.at[h], chip(0, 0, z + 4))
        sx, sy, t = spots[name]
        return remote(
            act.at[h], crossbuf.at[h], send_sem.at[h], cross_recv.at[h], chip(sx, sy, turn if t else z)
        )

    def cross_second(name, h):
        s = source_z if spots[name][2] else z
        return remote(crossbuf.at[h], prev.at[h], cross_send.at[h], prev_recv.at[h], chip(0, 0, s + 4))

    def first_sends(first):
        for h in range(first, first + SPAN):

            @pl.when(sends)
            def _(h=h):
                (long_first(LONG.index(h)) if h in LONG else direct(h)).start()

            @pl.when(is_source)
            def _(h=h):
                for name, taken in CROSS.items():
                    if h in taken:
                        cross_first(name, h).start()

    def long_pass(stage, k):
        @pl.when((first_relay, second_relay)[stage])
        def _():
            pltpu.make_async_copy(longbuf.at[stage, k], longbuf.at[stage, k], long_recv.at[stage, k]).wait()
            long_next(stage, k).start()

    def cross_pass(taken):
        for name, role in roles.items():
            mine = [h for h in taken if h in CROSS[name]]
            if mine:

                @pl.when(role)
                def _(name=name, mine=mine):
                    for h in mine:
                        pltpu.make_async_copy(crossbuf.at[h], crossbuf.at[h], cross_recv.at[h]).wait()
                        cross_second(name, h).start()

    def temporal(pair):
        @pl.when(gets)
        def _():
            for h in pair:
                pltpu.make_async_copy(prev.at[h], prev.at[h], prev_recv.at[h]).wait()

        rhs = stacked([[ref[h] for ref in (prev, even, act)] for h in pair])
        total = jnp.dot(tmat[...], rhs, preferred_element_type=F32).astype(BF16)
        for k, h in enumerate(pair):
            o_ref[h] = total[:, k * width : (k + 1) * width]

    finish(taps(*STEPS[0]), act, STEPS[0][1])
    first_sends(STEPS[0][1])
    za[...] = taps(*STEPS[1])
    here, there = za, zb
    for n in range(2, len(STEPS) + 1):
        if n < len(STEPS):
            if STEPS[n][1] in (0, rows - SPAN) and STEPS[n - 1][1] not in (0, rows - SPAN):
                halos[STEPS[n][0]].wait_recv()
            if STEPS[n][0] != STEPS[n - 1][0]:
                even_in.wait()
            there[...] = taps(*STEPS[n])
        else:
            wt_in.wait()
            at = 0
            for piece in turned_about([traw.at[k] for k in range(3)], bt_ref):
                tmat[:, at : at + piece.shape[1]] = piece
                at += piece.shape[1]
        i, h = STEPS[n - 1]
        finish(here[...], act if i else even, h)
        if i:
            first_sends(h)
        here, there = there, here
        for kind, what in BETWEEN.get(n, ()):
            if kind == "long":
                long_pass(*what)
            else:
                cross_pass(what)

    @pl.when(f == 0)
    def _():
        prev[...] = jnp.zeros_like(prev)

    gets = f != 0
    for kind, what in AFTER:
        if kind == "long":
            long_pass(*what)
        elif kind == "cross":
            cross_pass(what)
        else:

            @pl.when(jnp.logical_not(is_target))
            def _(what=what):
                temporal(what)

    @pl.when(is_target)
    def _():
        @pl.loop(0, rows // 2)
        def _(t):
            inner = jnp.logical_and(t >= 4, t < 6).astype(jnp.int32)
            h = 2 * t + 4 - 12 * inner - 4 * (t >= 6).astype(jnp.int32)
            temporal((h, h + 1))

    for i in range(2):
        halos[i].wait_send()

    @pl.when(sends)
    def _():
        for h in range(rows):
            direct(h).wait_send()

    @pl.when(is_source)
    def _():
        for h in range(rows):
            direct(h).wait_send()

    for stage, role in enumerate((first_relay, second_relay)):

        @pl.when(role)
        def _(stage=stage):
            for k in range(len(LONG)):
                long_next(stage, k).wait_send()

    for name, role in roles.items():
        for h in CROSS[name]:

            @pl.when(role)
            def _(name=name, h=h):
                cross_second(name, h).wait_send()


def per_device(video, w_spatial, b_spatial, w_temporal, b_temporal):
    frames, rows, width, channels = video.shape
    dma = pltpu.SemaphoreType.DMA
    out = pl.pallas_call(
        kernel,
        out_shape=pltpu.VMEM((rows, channels, width), BF16),
        in_specs=[
            pl.BlockSpec(memory_space=pl.ANY),
            pl.BlockSpec(memory_space=pl.ANY),
            pl.BlockSpec(memory_space=pltpu.VMEM),
            pl.BlockSpec(memory_space=pl.ANY),
            pl.BlockSpec(memory_space=pltpu.VMEM),
        ],
        out_specs=pl.BlockSpec(memory_space=pltpu.VMEM),
        scratch_shapes=[
            pltpu.VMEM((frames, rows + 2, channels, width), BF16),
            pltpu.VMEM(w_spatial.shape, BF16),
            pltpu.VMEM(w_temporal.shape, BF16),
            pltpu.VMEM((channels // GROUP, 3, GROUP, 3 * channels + ONES), BF16),
            pltpu.VMEM((channels, 3 * channels + ONES), BF16),
            pltpu.VMEM((rows, channels, width), BF16),
            pltpu.VMEM((rows, channels, width), BF16),
            pltpu.VMEM((rows, channels, width), BF16),
            pltpu.VMEM((3 * channels, SPAN * width), F32),
            pltpu.VMEM((3 * channels, SPAN * width), F32),
            pltpu.VMEM((2, len(LONG), channels, width), BF16),
            pltpu.VMEM((rows, channels, width), BF16),
            dma((6,)),
            dma((2,)),
            dma((2,)),
            dma((rows,)),
            dma((rows,)),
            dma((2, len(LONG))),
            dma((2, len(LONG))),
            dma((rows,)),
            dma((rows,)),
        ],
        compiler_params=pltpu.CompilerParams(
            collective_id=0, has_side_effects=True, vmem_limit_bytes=60 * 1024 * 1024
        ),
        name="level",
    )(
        jnp.swapaxes(video, 2, 3),
        w_spatial,
        b_spatial,
        w_temporal,
        b_temporal,
    )
    return jnp.swapaxes(out, 1, 2)[None]


def solution(mesh):
    in_specs = (P(("batch", "frames"), "rows", None, None), P(), P(), P(), P())
    out_specs = P(("batch", "frames"), "rows", None, None)
    return jax.shard_map(
        per_device, mesh=mesh, in_specs=in_specs, out_specs=out_specs, check_vma=False
    )
```
